32 devices in a mesh: lat: 8 (over y, x, core), lon: 4 (over z).
Axes of the slice: x: 2, y: 2, z: 4, core: 2. Of those that a mesh axis runs over, the one named last changes fastest.
Arguments:
- adjoint_in: float32 [2, 24, 128, 2880], P(None, None, 'lat', 'lon'), may hold values from -6 to 6
- wind_east: float32 [24, 128, 2880], P(None, 'lat', 'lon'), may hold values from -0.45 to 0.45
- wind_north: float32 [24, 128, 2880], P(None, 'lat', 'lon'), may hold values from -0.45 to 0.45
- polar_mask: int32 [128], replicated, may hold values from 0 to 1, as said below
- obs_owner: int32 [131072, 1], P(('lat', 'lon')), may hold values from 0 to 31; in each aligned block of 4096 rows (0 to 4095, 4096 to 8191, ...) at most 256 rows name the same one
- obs_cell: int32 [131072], P(('lat', 'lon')), may hold values from 0 to 11519
- obs_kernel: float32 [131072, 24], P(('lat', 'lon')), may hold values from 0.2 to 2
- obs_resid: float32 [131072, 2], P(('lat', 'lon')), may hold values from -6 to 6
Outputs:
- adjoint_out: float32 [2, 24, 128, 2880], P(None, None, 'lat', 'lon')
The draws below stay inside these ranges and needn't reach their ends.
Inputs may be any that keep to these rules, and one draw needn't show every extreme that they name: polar_mask is 1 exactly on the first KS rows and the last KN rows, with KS and KN each from 1 to 16 and one of them equal to 16. `obs_owner`: among the soundings of one device no owner is named more than 256 times, and in every draw some device names some owner exactly 256 times.
All inputs are finite; a program needn't handle non-finite values.
Results may differ from the reference program's by a relative error of at most 0.00008.
Values sent between devices are 32-bit elements; how exact they have to be, the bound alone decides.
A program may use at most 128 MiB of HBM per device.

```python
import math
import jax
import jax.numpy as jnp
import numpy as np

NLON = 2880
TRACERS = 2
LEV = 24
LAT_DEV = 16
OBS_DEV = 4096
LON_DEV = 720
NLAT = 128
POLAR_MAX = 16
CAP = 256
NOBS = 131072
N_LON = 4
DEVICES = 32


def draw_polar_mask(key, part):
    key_side = jax.random.fold_in(key, 11)
    key_count = jax.random.fold_in(key, 23)
    other_count = jax.random.randint(key_count, (), 1, POLAR_MAX + 1)
    flipped = jax.random.randint(key_side, (), 0, 2)
    north_count = jnp.where(flipped == 1, POLAR_MAX, other_count)
    south_count = jnp.where(flipped == 1, other_count, POLAR_MAX)
    row_ids = jnp.arange(NLAT)
    return ((row_ids < south_count) | (row_ids >= NLAT - north_count)).astype(jnp.int32)


def set_ends(array, stream_key, smallest, high):
    extent = array.shape
    index_at = [jax.random.randint(jax.random.fold_in(stream_key, axis), (), 0, extent[axis]) for axis in range(len(extent))]
    array = array.at[tuple(index_at)].set(smallest)
    longest = extent.index(max(extent))
    index_at[longest] = (index_at[longest] + 1) % extent[longest]
    return array.at[tuple(index_at)].set(high)


def block_scale(stream_key, extent, shards, least, top_value):
    gain, own = 1.0, jax.random.fold_in(stream_key, 6)
    for dim, blocks in shards:
        heights = jnp.exp(jax.random.uniform(jax.random.fold_in(own, dim), (blocks,), jnp.float32, least / len(shards), top_value / len(shards)))
        gain = gain * jnp.repeat(heights, extent[dim] // blocks).reshape([-1 if axis == dim else 1 for axis in range(len(extent))])
    return gain


def routed_block(own_key, own, number, rows, number_of, top, most, lean):
    sequence = jax.random.permutation(own_key, number_of)
    crowded, usual = portions_of(number_of, rows * top, most, lean, True), portions_of(number_of, rows * top, most, lean, False)
    places = jnp.arange(number_of)

    def named(sizes, rotation):
        used = int((sizes > 0).sum())
        fixed = max(1, used // 4)
        moved = fixed + (places - fixed + rotation * (used - fixed)) % max(1, number_of - fixed)
        return jnp.zeros((number_of,), jnp.int32).at[sequence[jnp.where(places < fixed, places, moved)]].set(jnp.asarray(sizes, jnp.int32))

    sizes = jnp.where(number % 4 == 0, named(crowded, number // 4), named(usual, number - number // 4 - 1))
    mixed = jax.random.permutation(jax.random.fold_in(own, 3), number_of)
    donor, sink = mixed[0:number_of // 2 * 2:2], mixed[1:number_of // 2 * 2:2]
    margin = jnp.minimum(sizes[donor] - 1, most - sizes[sink]) // 2
    margin = jnp.where((donor == sequence[0]) | (sink == sequence[0]) | (sizes[sink] == 0), 0, jnp.maximum(margin, 0))
    moved = jax.random.randint(jax.random.fold_in(own, 4), (number_of // 2,), 0, 1 << 20) % (margin + 1)
    sizes = sizes.at[donor].add(-moved).at[sink].add(moved)
    members = jnp.searchsorted(jnp.cumsum(sizes), jnp.arange(rows * top), side="right").astype(jnp.int32)
    listing = members.reshape(top, rows).T
    listing = listing[jax.random.permutation(jax.random.fold_in(own, 1), rows)]
    rotation = jax.random.randint(jax.random.fold_in(own, 2), (rows, 1), 0, top)
    return jnp.take_along_axis(listing, (jnp.arange(top)[None, :] + rotation) % top, axis=1)


def portions_of(amount, total, reach, lean, full):
    portions = [(1 << 20) // math.isqrt(rank ** lean) + 1 for rank in range(1, amount + 1)]
    largest = reach if full else min(reach, max(-(-total // amount), total * portions[0] // sum(portions)))
    least = 1 if total - largest >= amount - 1 else 0
    counts, spare = [largest] + [least] * (amount - 1), total - largest - least * (amount - 1)
    while spare > 0:
        candidates = [i for i in range(1, amount) if counts[i] < largest] or [i for i in range(1, amount) if counts[i] < reach]
        pool, left = sum([portions[i] for i in candidates]), spare
        for i in candidates:
            extra = min(reach - counts[i], max(1, left * portions[i] // pool), spare)
            counts[i] = counts[i] + extra
            spare = spare - extra
    return np.array(counts)


def noise(stream_key, dims, deviation, bound, pieces=(), held_as=jnp.bfloat16):
    entries = jax.random.normal(stream_key, dims, jnp.float32) * deviation
    if len(pieces) > 0:
        entries = block_scale(stream_key, dims, pieces, -0.22, 0.18) * entries
    return jnp.clip(entries, min=-bound, max=bound).astype(held_as)


def setup_inputs(seed: int = 0) -> dict:
    key_list = jax.random.split(jax.random.key(seed), 9)
    adjoint_in = noise(key_list[0], (TRACERS, LEV, NLAT, NLON), 1.0, 6.0, ((2, 8), (3, 4)), jnp.float32)
    wind_east = jnp.clip(jax.random.uniform(key_list[1], (LEV, NLAT, NLON), jnp.float32, -0.45, 0.45) * block_scale(key_list[1], (LEV, NLAT, NLON), ((1, 8), (2, 4)), -0.4, 0.0), -0.45, 0.45)
    wind_north = jnp.clip(jax.random.uniform(key_list[2], (LEV, NLAT, NLON), jnp.float32, -0.45, 0.45) * block_scale(key_list[2], (LEV, NLAT, NLON), ((1, 8), (2, 4)), -0.4, 0.0), -0.45, 0.45)
    polar_mask = draw_polar_mask(jax.random.fold_in(key_list[8], 71), 0)
    obs_owner_keys = jax.random.split(jax.random.fold_in(key_list[4], 1), NOBS // OBS_DEV)
    obs_owner_turns = jax.random.permutation(jax.random.fold_in(key_list[4], 3), NOBS // OBS_DEV)
    obs_owner = jax.vmap(lambda own, number: routed_block(jax.random.fold_in(key_list[4], 2), own, number, OBS_DEV, DEVICES, 1, CAP, 2))(obs_owner_keys, obs_owner_turns).reshape((NOBS, 1))
    obs_cell = set_ends(jax.random.randint(key_list[5], (NOBS,), 0, LAT_DEV * LON_DEV), jax.random.fold_in(key_list[5], 1), 0, (LAT_DEV * LON_DEV) - 1).astype(jnp.int32)
    obs_kernel = jnp.clip(jnp.exp(math.log(2.0) - 2.3025851 * jax.random.uniform(key_list[6], (NOBS, LEV), jnp.float32) ** block_scale(key_list[6], (NOBS, LEV), ((0, 32),), -0.2, 0.2)), 0.2, 2.0)
    obs_resid = noise(key_list[7], (NOBS, TRACERS), 1.0, 6.0, ((0, 32),), jnp.float32)
    return dict(adjoint_in=adjoint_in, wind_east=wind_east, wind_north=wind_north, polar_mask=polar_mask, obs_owner=obs_owner, obs_cell=obs_cell, obs_kernel=obs_kernel, obs_resid=obs_resid)


def route_forcing(adjoint_in, obs_owner, obs_cell, obs_kernel, obs_resid):
    lon_dev = NLON // N_LON
    owner_dev = obs_owner[:, 0]
    row_ids = (owner_dev // N_LON) * LAT_DEV + obs_cell // lon_dev
    col_ids = (owner_dev % N_LON) * lon_dev + obs_cell % lon_dev
    flat_index = (row_ids * NLON + col_ids).astype(jnp.int32)
    contrib = obs_resid[:, :, None] * obs_kernel[:, None, :]
    contrib = contrib.reshape(contrib.shape[0], TRACERS * LEV)
    adjoint = adjoint_in.reshape(TRACERS * LEV, NLAT * NLON)
    adjoint = adjoint.at[:, flat_index].add(contrib.T)
    return adjoint.reshape(TRACERS, LEV, NLAT, NLON)


def polar_filter(adjoint, polar_mask):
    row_ids = jnp.arange(NLAT)
    cosine = jnp.sin(math.pi * (row_ids + 0.5) / NLAT)
    lat_ratio = cosine / math.sin(math.pi * POLAR_MAX / NLAT)
    wavenum = jnp.arange(NLON // 2 + 1)
    sine_k = jnp.sin(math.pi * wavenum / NLON)
    damping = lat_ratio[:, None] / jnp.maximum(sine_k[None, :], lat_ratio[:, None])
    damping = jnp.where(polar_mask[:, None] > 0, damping, 1.0)
    spectra = jnp.fft.rfft(adjoint, axis=-1)
    return jnp.fft.irfft(spectra * damping[None, None], n=NLON, axis=-1)


def adjoint_advect(adjoint, wind_east, wind_north):
    row_ids = jnp.arange(NLAT)
    north_wind = jnp.where(row_ids[None, :, None] < NLAT - 1, wind_north, 0.0)
    east_face = jnp.maximum(wind_east, 0.0)
    west_face = jnp.minimum(jnp.roll(wind_east, 1, axis=-1), 0.0)
    north_face = jnp.maximum(north_wind, 0.0)
    south_wind = jnp.concatenate([jnp.zeros_like(north_wind[:, :1]), north_wind[:, :-1]], axis=1)
    south_face = jnp.minimum(south_wind, 0.0)
    east_val = jnp.roll(adjoint, -1, axis=-1)
    west_val = jnp.roll(adjoint, 1, axis=-1)
    zero_row = jnp.zeros_like(adjoint[:, :, :1])
    upper_val = jnp.concatenate([adjoint[:, :, 1:], zero_row], axis=2)
    lower_val = jnp.concatenate([zero_row, adjoint[:, :, :-1]], axis=2)
    result = adjoint + east_face * (east_val - adjoint) + west_face * (adjoint - west_val)
    return result + north_face * (upper_val - adjoint) + south_face * (adjoint - lower_val)


def reference(adjoint_in, wind_east, wind_north, polar_mask, obs_owner, obs_cell, obs_kernel, obs_resid):
    forced = route_forcing(adjoint_in, obs_owner, obs_cell, obs_kernel, obs_resid)
    filtered = polar_filter(forced, polar_mask)
    return adjoint_advect(filtered, wind_east, wind_north)
```

```python
import functools
import math

import jax
import jax.numpy as jnp
import numpy as np
from jax import lax
from jax.experimental import pallas as pl
from jax.experimental.pallas import tpu as pltpu
from jax.sharding import PartitionSpec as P

precise_mode = lax.Precision.HIGH
ACCS = 4
UNROLL = 4


def circle_tables(lon_width):
    width = lon_width // 4
    half = width // 2
    inner = 16

    def table(waves, turns, repeats):
        high = np.arange(width // inner)[:, None] * inner
        high = 2.0 * np.pi * ((high * waves[None, :]) % lon_width) / lon_width
        high = np.concatenate([high + 0.5 * np.pi * turn for turn in range(repeats)], 0)
        low = np.arange(inner)[:, None]
        low = 2.0 * np.pi * ((low * waves[None, :]) % lon_width) / lon_width
        low = low - 0.5 * np.pi * turns[None, :]
        parts = [np.cos(high), np.sin(high), np.cos(low), np.sin(low)]
        parts = lax.optimization_barrier([jnp.asarray(part.astype(np.float32)) for part in parts])
        cos_high, sin_high, cos_low, sin_low = parts
        full = cos_high[:, None] * cos_low[None] - sin_high[:, None] * sin_low[None]
        return full.reshape(repeats * width, waves.shape[0])

    zero = np.concatenate([4 * np.arange(half + 1), 4 * np.arange(1, half)])
    zero_turns = np.concatenate([np.zeros(half + 1), np.ones(half - 1)])
    zero_weights = np.where((zero == 0) | (zero == lon_width // 2), 1.0, 2.0)
    two = np.tile(4 * np.arange(half) + 2, 2)
    one = np.tile(4 * np.arange(width) + 1, 2)
    return [
        (table(zero, zero_turns, 1), zero, zero_weights / lon_width),
        (table(two, np.repeat([0, 1], half), 1), two, np.full(width, 2.0 / lon_width)),
        (table(one, np.repeat([0, 1], width), 2), one, np.full(2 * width, 2.0 / lon_width)),
    ]


def corrected(data, basis, waves, weights, lat_ratio, live, lon_width):
    fields, rows, width = data.shape
    sine_k = jnp.asarray(np.sin(np.pi * waves / lon_width).astype(np.float32))
    damping = lat_ratio[:, None] / jnp.maximum(sine_k[None, :], lat_ratio[:, None])
    factor = (damping - 1.0) * jnp.asarray(weights.astype(np.float32))[None, :]
    factor = jnp.where(live[:, None], factor, 0.0)
    spectra = jnp.dot(data.reshape(fields * rows, width), basis, precision=precise_mode)
    spectra = (spectra.reshape(fields, rows, width) * factor[None]).reshape(fields * rows, width)
    result = lax.dot_general(spectra, basis, (((1,), (1,)), ((), ())), precision=precise_mode)
    return result.reshape(fields, rows, width)


def scatter_kernel(cells_ref, values_ref, out_ref, *extra):
    accs = (out_ref,) + extra
    total, width = out_ref.shape
    chunk = 64
    count = values_ref.shape[0]

    def clear(i, carry):
        where = pl.ds(pl.multiple_of(i * chunk, chunk), chunk)
        for acc in accs:
            acc[where, :] = jnp.zeros((chunk, width), jnp.float32)
        return carry

    lax.fori_loop(0, total // chunk, clear, 0)
    step = ACCS * UNROLL

    def add(i, carry):
        base = i * step
        for turn in range(UNROLL):
            places, olds = [], []
            for lane in range(ACCS):
                place = cells_ref[base + turn * ACCS + lane]
                places.append(place)
                olds.append(
                    accs[lane][pl.ds(place, 1), :]
                    + values_ref[pl.ds(base + turn * ACCS + lane, 1), :]
                )
            for lane in range(ACCS):
                accs[lane][pl.ds(places[lane], 1), :] = olds[lane]
        return carry

    lax.fori_loop(0, count // step, add, 0)

    def join(i, carry):
        where = pl.ds(pl.multiple_of(i * chunk, chunk), chunk)
        total_here = accs[0][where, :]
        for acc in extra:
            total_here = total_here + acc[where, :]
        out_ref[where, :] = total_here
        return carry

    lax.fori_loop(0, total // chunk, join, 0)


def add_soundings(cells, values, total):
    width = values.shape[1]
    return pl.pallas_call(
        scatter_kernel,
        out_shape=jax.ShapeDtypeStruct((total, width), jnp.float32),
        in_specs=[
            pl.BlockSpec(memory_space=pltpu.SMEM),
            pl.BlockSpec(memory_space=pltpu.VMEM),
        ],
        out_specs=pl.BlockSpec(memory_space=pltpu.VMEM),
        scratch_shapes=[pltpu.VMEM((total, width), jnp.float32)] * (ACCS - 1),
        compiler_params=pltpu.CompilerParams(vmem_limit_bytes=48 * 1024 * 1024),
    )(cells, values)


def stencil_kernel(
    field_ref, east_ref, north_ref, east_col, west_col, north_row, south_row,
    wind_col, wind_row, out_ref, wide,
):
    tracers, levels, rows, width = field_ref.shape
    padded = wide.shape[1]
    lanes = lax.broadcasted_iota(jnp.int32, (rows, padded), 1)
    subs = lax.broadcasted_iota(jnp.int32, (rows, padded), 0)

    def widened(slot, block):
        wide[slot * rows : (slot + 1) * rows, 0:width] = block
        return wide[slot * rows : (slot + 1) * rows, :]

    def wide_row(slot, block):
        wide[slot * rows : slot * rows + 1, 0:width] = block
        return wide[slot * rows : slot * rows + 1, :]

    for level in range(levels):
        wind_east = widened(0, east_ref[level])
        wind_west = jnp.where(lanes == 0, wind_col[level], pltpu.roll(wind_east, 1, 1))
        wind_north = widened(1, north_ref[level])
        wind_south = jnp.where(
            subs == 0, wide_row(2, wind_row[level]), pltpu.roll(wind_north, 1, 0)
        )
        east_face = jnp.maximum(wind_east, 0.0)
        west_face = jnp.minimum(wind_west, 0.0)
        north_face = jnp.maximum(wind_north, 0.0)
        south_face = jnp.minimum(wind_south, 0.0)
        for tracer in range(tracers):
            center = widened(3 + 3 * tracer, field_ref[tracer, level])
            east_val = jnp.where(
                lanes == width - 1, east_col[tracer, level], pltpu.roll(center, padded - 1, 1)
            )
            west_val = jnp.where(lanes == 0, west_col[tracer, level], pltpu.roll(center, 1, 1))
            upper_val = jnp.where(
                subs == rows - 1,
                wide_row(4 + 3 * tracer, north_row[tracer, level]),
                pltpu.roll(center, rows - 1, 0),
            )
            lower_val = jnp.where(
                subs == 0,
                wide_row(5 + 3 * tracer, south_row[tracer, level]),
                pltpu.roll(center, 1, 0),
            )
            result = center + east_face * (east_val - center) + west_face * (center - west_val)
            result = result + north_face * (upper_val - center) + south_face * (center - lower_val)
            out_ref[tracer, level] = result[:, 0:width]


def advect(field, wind_east, wind_north, east_col, west_col, north_row, south_row, wind_col, wind_row):
    tracers, levels, rows, width = field.shape
    step = 4 if levels % 4 == 0 else 1

    def four(depth, span):
        return pl.BlockSpec((tracers, step, depth, span), lambda i: (0, i, 0, 0))

    def three(depth, span):
        return pl.BlockSpec((step, depth, span), lambda i: (i, 0, 0))

    padded = -(-(width + 1) // 128) * 128
    return pl.pallas_call(
        stencil_kernel,
        grid=(levels // step,),
        out_shape=jax.ShapeDtypeStruct(field.shape, jnp.float32),
        in_specs=[
            four(rows, width), three(rows, width), three(rows, width),
            four(rows, 1), four(rows, 1), four(1, width), four(1, width),
            three(rows, 1), three(1, width),
        ],
        out_specs=four(rows, width),
        scratch_shapes=[pltpu.VMEM(((3 + 3 * tracers) * rows, padded), jnp.float32)],
        compiler_params=pltpu.CompilerParams(vmem_limit_bytes=32 * 1024 * 1024),
    )(field, wind_east, wind_north, east_col, west_col, north_row, south_row, wind_col, wind_row)


def owner_positions(owner_dev, devices):
    count = owner_dev.shape[0]
    span = 128
    one_hot = (owner_dev[:, None] == lax.broadcasted_iota(jnp.int32, (1, devices), 1)).astype(
        jnp.bfloat16
    ).reshape(count // span, span, devices)
    lower = jnp.asarray(np.tril(np.ones((span, span))), jnp.bfloat16)
    inner = jnp.einsum("ij,bjd->bid", lower, one_hot, preferred_element_type=jnp.float32)
    sums = inner[:, -1, :]
    blocks = count // span
    before = jnp.asarray(np.tril(np.ones((blocks, blocks)), -1), jnp.float32)
    offset = jnp.dot(before, sums, precision=lax.Precision.HIGHEST)
    ranks = (inner + offset[:, None, :]) * one_hot.astype(jnp.float32)
    return jnp.sum(ranks, axis=2).reshape(count).astype(jnp.int32) - 1


def shards(
    adjoint_in, wind_east, wind_north, polar_mask, obs_owner, obs_cell, obs_kernel, obs_resid
):
    tracers, levels, lat_dev, lon_dev = adjoint_in.shape
    fields = tracers * levels
    lat_count = lax.axis_size("lat")
    lon_count = lax.axis_size("lon")
    lat_index = lax.axis_index("lat")
    lon_width = lon_dev * lon_count
    total_rows = lat_dev * lat_count
    devices = lat_count * lon_count
    obs_count = obs_owner.shape[0]
    capacity = 2 * obs_count // devices

    owner_dev = obs_owner[:, 0]
    slot_index = owner_dev * capacity + owner_positions(owner_dev, devices)
    payload = jnp.concatenate(
        [
            obs_kernel,
            obs_resid,
            obs_cell.astype(jnp.float32)[:, None],
            jnp.zeros((obs_count, 32 - levels - tracers - 1), jnp.float32),
        ],
        axis=1,
    )
    send = jnp.zeros((devices * capacity, 32), jnp.float32).at[slot_index].set(
        payload, unique_indices=True
    )
    got = lax.all_to_all(
        send.reshape(devices, capacity, 32), ("lat", "lon"), split_axis=0, concat_axis=0, tiled=True
    ).reshape(devices * capacity, 32)
    got_cells = got[:, levels + tracers].astype(jnp.int32)
    got_values = (
        got[:, levels : levels + tracers, None] * got[:, None, :levels]
    ).reshape(devices * capacity, fields)
    forcing = add_soundings(got_cells, got_values, lat_dev * lon_dev)
    adjoint = (
        adjoint_in.reshape(fields, lat_dev, lon_dev)
        + forcing.T.reshape(fields, lat_dev, lon_dev)
    )

    local_rows = lat_index * lat_dev + jnp.arange(lat_dev, dtype=jnp.int32)
    north_wind = jnp.where(local_rows[None, :, None] < total_rows - 1, wind_north, 0.0)
    up = [(i, i + 1) for i in range(lat_count - 1)]
    down = [(i + 1, i) for i in range(lat_count - 1)]
    east = [(i, (i + 1) % lon_count) for i in range(lon_count)]
    west = [((i + 1) % lon_count, i) for i in range(lon_count)]
    wind_row = lax.ppermute(north_wind[:, -1, :], "lat", up)[:, None, :]
    wind_col = lax.ppermute(wind_east[:, :, -1], "lon", east)[:, :, None]

    grouped = lax.all_to_all(
        adjoint.reshape(lon_count, fields // lon_count, lat_dev, lon_dev),
        "lon", split_axis=0, concat_axis=0, tiled=True,
    )
    lat_ratio = jnp.sin(math.pi * (local_rows.astype(jnp.float32) + 0.5) / total_rows) / math.sin(
        math.pi * (total_rows // 8) / total_rows
    )
    live = lax.dynamic_slice_in_dim(polar_mask, lat_index * lat_dev, lat_dev) > 0
    tables = circle_tables(lon_width)
    blocks = lon_count // 4
    quarters = [
        jnp.concatenate([grouped[blocks * i + j] for j in range(blocks)], axis=2) for i in range(4)
    ]
    quarter = lon_dev * blocks
    sum_even, sum_odd = quarters[0] + quarters[2], quarters[1] + quarters[3]
    pair = jnp.concatenate([quarters[0] - quarters[2], quarters[1] - quarters[3]], axis=2)
    filt = functools.partial(corrected, lat_ratio=lat_ratio, live=live, lon_width=lon_width)
    zero_part = filt(sum_even + sum_odd, *tables[0])
    two_part = filt(sum_even - sum_odd, *tables[1])
    pair_part = filt(pair, *tables[2])
    first, second = pair_part[:, :, :quarter], pair_part[:, :, quarter:]
    even_part, odd_part = zero_part + two_part, zero_part - two_part
    results = [
        quarters[0] + (even_part + first),
        quarters[1] + (odd_part + second),
        quarters[2] + (even_part - first),
        quarters[3] + (odd_part - second),
    ]
    filtered = jnp.stack(
        [
            result[:, :, j * lon_dev : (j + 1) * lon_dev]
            for result in results
            for j in range(blocks)
        ]
    )
    field = lax.all_to_all(filtered, "lon", split_axis=0, concat_axis=0, tiled=True)
    field = field.reshape(tracers, levels, lat_dev, lon_dev)

    north_row = lax.ppermute(field[:, :, 0, :], "lat", down)[:, :, None, :]
    south_row = lax.ppermute(field[:, :, -1, :], "lat", up)[:, :, None, :]
    east_col = lax.ppermute(field[:, :, :, 0], "lon", west)[..., None]
    west_col = lax.ppermute(field[:, :, :, -1], "lon", east)[..., None]
    return advect(
        field, wind_east, north_wind, east_col, west_col, north_row, south_row, wind_col, wind_row
    )


def solution(mesh):
    placed = (
        P(None, None, "lat", "lon"),
        P(None, "lat", "lon"),
        P(None, "lat", "lon"),
        P(),
        P(("lat", "lon"), None),
        P(("lat", "lon")),
        P(("lat", "lon"), None),
        P(("lat", "lon"), None),
    )

    return jax.shard_map(
        shards, mesh=mesh, in_specs=placed, out_specs=P(None, None, "lat", "lon"), check_vma=False
    )
```

```python
import functools
import math

import jax
import jax.numpy as jnp
import numpy as np
from jax import lax
from jax.experimental import pallas as pl
from jax.experimental.pallas import tpu as pltpu
from jax.sharding import PartitionSpec as P

precise_mode = lax.Precision.HIGH
ACCS = 4
UNROLL = 4


def circle_tables(lon_width):
    width = lon_width // 4
    half = width // 2
    inner = 16

    def table(waves, turns, repeats):
        high = np.arange(width // inner)[:, None] * inner
        high = 2.0 * np.pi * ((high * waves[None, :]) % lon_width) / lon_width
        high = np.concatenate([high + 0.5 * np.pi * turn for turn in range(repeats)], 0)
        low = np.arange(inner)[:, None]
        low = 2.0 * np.pi * ((low * waves[None, :]) % lon_width) / lon_width
        low = low - 0.5 * np.pi * turns[None, :]
        parts = [np.cos(high), np.sin(high), np.cos(low), np.sin(low)]
        parts = lax.optimization_barrier([jnp.asarray(part.astype(np.float32)) for part in parts])
        cos_high, sin_high, cos_low, sin_low = parts
        full = cos_high[:, None] * cos_low[None] - sin_high[:, None] * sin_low[None]
        return full.reshape(repeats * width, waves.shape[0])

    zero = np.concatenate([4 * np.arange(half + 1), 4 * np.arange(1, half)])
    zero_turns = np.concatenate([np.zeros(half + 1), np.ones(half - 1)])
    zero_weights = np.where((zero == 0) | (zero == lon_width // 2), 1.0, 2.0)
    two = np.tile(4 * np.arange(half) + 2, 2)
    one = np.tile(4 * np.arange(width) + 1, 2)
    return [
        (table(zero, zero_turns, 1), zero, zero_weights / lon_width),
        (table(two, np.repeat([0, 1], half), 1), two, np.full(width, 2.0 / lon_width)),
        (table(one, np.repeat([0, 1], width), 2), one, np.full(2 * width, 2.0 / lon_width)),
    ]


def corrected(data, basis, waves, weights, lat_ratio, live, lon_width):
    fields, rows, width = data.shape
    sine_k = jnp.asarray(np.sin(np.pi * waves / lon_width).astype(np.float32))
    damping = lat_ratio[:, None] / jnp.maximum(sine_k[None, :], lat_ratio[:, None])
    factor = (damping - 1.0) * jnp.asarray(weights.astype(np.float32))[None, :]
    factor = jnp.where(live[:, None], factor, 0.0)
    spectra = jnp.dot(data.reshape(fields * rows, width), basis, precision=precise_mode)
    spectra = (spectra.reshape(fields, rows, width) * factor[None]).reshape(fields * rows, width)
    result = lax.dot_general(spectra, basis, (((1,), (1,)), ((), ())), precision=precise_mode)
    return result.reshape(fields, rows, width)


def scatter_kernel(cells_ref, values_ref, out_ref, *extra):
    accs = (out_ref,) + extra
    total, width = out_ref.shape
    chunk = 64
    count = values_ref.shape[0]

    def clear(i, carry):
        where = pl.ds(pl.multiple_of(i * chunk, chunk), chunk)
        for acc in accs:
            acc[where, :] = jnp.zeros((chunk, width), jnp.float32)
        return carry

    lax.fori_loop(0, total // chunk, clear, 0)
    step = ACCS * UNROLL

    def add(i, carry):
        base = i * step
        for turn in range(UNROLL):
            places, olds = [], []
            for lane in range(ACCS):
                place = cells_ref[base + turn * ACCS + lane]
                places.append(place)
                olds.append(
                    accs[lane][pl.ds(place, 1), :]
                    + values_ref[pl.ds(base + turn * ACCS + lane, 1), :]
                )
            for lane in range(ACCS):
                accs[lane][pl.ds(places[lane], 1), :] = olds[lane]
        return carry

    lax.fori_loop(0, count // step, add, 0)

    def join(i, carry):
        where = pl.ds(pl.multiple_of(i * chunk, chunk), chunk)
        total_here = accs[0][where, :]
        for acc in extra:
            total_here = total_here + acc[where, :]
        out_ref[where, :] = total_here
        return carry

    lax.fori_loop(0, total // chunk, join, 0)


def add_soundings(cells, values, total):
    width = values.shape[1]
    return pl.pallas_call(
        scatter_kernel,
        out_shape=jax.ShapeDtypeStruct((total, width), jnp.float32),
        in_specs=[
            pl.BlockSpec(memory_space=pltpu.SMEM),
            pl.BlockSpec(memory_space=pltpu.VMEM),
        ],
        out_specs=pl.BlockSpec(memory_space=pltpu.VMEM),
        scratch_shapes=[pltpu.VMEM((total, width), jnp.float32)] * (ACCS - 1),
        compiler_params=pltpu.CompilerParams(vmem_limit_bytes=48 * 1024 * 1024),
    )(cells, values)


def stencil_kernel(keep_ref, field_ref, east_ref, north_ref, cols_ref, rows_ref, out_ref, wide, edge):
    tracers, levels, rows, width = field_ref.shape
    padded = wide.shape[1]
    lanes = lax.broadcasted_iota(jnp.int32, (rows, padded), 1)
    subs = lax.broadcasted_iota(jnp.int32, (rows, padded), 0)
    keep = keep_ref[0]

    def widened(slot, block):
        wide[slot * rows : (slot + 1) * rows, 0:width] = block
        return wide[slot * rows : (slot + 1) * rows, :]

    for level in range(levels):
        cols = cols_ref[level]
        edge[0 : 2 * tracers + 1, 0:width] = rows_ref[level]
        wind_east = widened(0, east_ref[level])
        wind_west = jnp.where(
            lanes == 0, cols[:, 2 * tracers : 2 * tracers + 1], pltpu.roll(wind_east, 1, 1)
        )
        wind_north = widened(1, north_ref[level])
        wind_south = jnp.where(
            subs == 0, edge[2 * tracers : 2 * tracers + 1, :], pltpu.roll(wind_north, 1, 0)
        )
        wind_north = jnp.where((subs == rows - 1) & (keep == 0), 0.0, wind_north)
        east_face = jnp.maximum(wind_east, 0.0)
        west_face = jnp.minimum(wind_west, 0.0)
        north_face = jnp.maximum(wind_north, 0.0)
        south_face = jnp.minimum(wind_south, 0.0)
        for tracer in range(tracers):
            other = tracers + tracer
            center = widened(2 + tracer, field_ref[tracer, level])
            east_val = jnp.where(
                lanes == width - 1, cols[:, tracer : tracer + 1], pltpu.roll(center, padded - 1, 1)
            )
            west_val = jnp.where(lanes == 0, cols[:, other : other + 1], pltpu.roll(center, 1, 1))
            upper_val = jnp.where(
                subs == rows - 1, edge[tracer : tracer + 1, :], pltpu.roll(center, rows - 1, 0)
            )
            lower_val = jnp.where(subs == 0, edge[other : other + 1, :], pltpu.roll(center, 1, 0))
            result = center + east_face * (east_val - center) + west_face * (center - west_val)
            result = result + north_face * (upper_val - center) + south_face * (center - lower_val)
            out_ref[tracer, level] = result[:, 0:width]


def advect(keep, field, wind_east, wind_north, cols, rows_edge):
    tracers, levels, rows, width = field.shape
    step = 4 if levels % 4 == 0 else 1
    padded = -(-(width + 1) // 128) * 128
    edges = 2 * tracers + 1

    def four(depth, span):
        return pl.BlockSpec((tracers, step, depth, span), lambda i: (0, i, 0, 0))

    def three(depth, span):
        return pl.BlockSpec((step, depth, span), lambda i: (i, 0, 0))

    return pl.pallas_call(
        stencil_kernel,
        grid=(levels // step,),
        out_shape=jax.ShapeDtypeStruct(field.shape, jnp.float32),
        in_specs=[
            pl.BlockSpec(memory_space=pltpu.SMEM),
            four(rows, width), three(rows, width), three(rows, width),
            three(rows, edges), three(edges, width),
        ],
        out_specs=four(rows, width),
        scratch_shapes=[
            pltpu.VMEM(((2 + tracers) * rows, padded), jnp.float32),
            pltpu.VMEM((8, padded), jnp.float32),
        ],
        compiler_params=pltpu.CompilerParams(vmem_limit_bytes=32 * 1024 * 1024),
    )(keep, field, wind_east, wind_north, cols, rows_edge)


def owner_positions(owner_dev, devices):
    count = owner_dev.shape[0]
    span = 128
    one_hot = (owner_dev[:, None] == lax.broadcasted_iota(jnp.int32, (1, devices), 1)).astype(
        jnp.bfloat16
    ).reshape(count // span, span, devices)
    lower = jnp.asarray(np.tril(np.ones((span, span))), jnp.bfloat16)
    inner = jnp.einsum("ij,bjd->bid", lower, one_hot, preferred_element_type=jnp.float32)
    sums = inner[:, -1, :]
    blocks = count // span
    before = jnp.asarray(np.tril(np.ones((blocks, blocks)), -1), jnp.float32)
    offset = jnp.dot(before, sums, precision=lax.Precision.HIGHEST)
    ranks = (inner + offset[:, None, :]) * one_hot.astype(jnp.float32)
    return jnp.sum(ranks, axis=2).reshape(count).astype(jnp.int32) - 1


def shards(
    adjoint_in, wind_east, wind_north, polar_mask, obs_owner, obs_cell, obs_kernel, obs_resid
):
    tracers, levels, lat_dev, lon_dev = adjoint_in.shape
    fields = tracers * levels
    lat_count = lax.axis_size("lat")
    lon_count = lax.axis_size("lon")
    lat_index = lax.axis_index("lat")
    lon_width = lon_dev * lon_count
    total_rows = lat_dev * lat_count
    devices = lat_count * lon_count
    obs_count = obs_owner.shape[0]
    capacity = 2 * obs_count // devices

    owner_dev = obs_owner[:, 0]
    slot_index = owner_dev * capacity + owner_positions(owner_dev, devices)
    payload = jnp.concatenate(
        [
            obs_kernel,
            obs_resid,
            obs_cell.astype(jnp.float32)[:, None],
            jnp.zeros((obs_count, 32 - levels - tracers - 1), jnp.float32),
        ],
        axis=1,
    )
    send = jnp.zeros((devices * capacity, 32), jnp.float32).at[slot_index].set(
        payload, unique_indices=True
    )
    got = lax.all_to_all(
        send.reshape(devices, capacity, 32), ("lat", "lon"), split_axis=0, concat_axis=0, tiled=True
    ).reshape(devices * capacity, 32)
    got_cells = got[:, levels + tracers].astype(jnp.int32)
    got_values = (
        got[:, levels : levels + tracers, None] * got[:, None, :levels]
    ).reshape(devices * capacity, fields)
    forcing = add_soundings(got_cells, got_values, lat_dev * lon_dev)
    adjoint = (
        adjoint_in.reshape(fields, lat_dev, lon_dev)
        + forcing.T.reshape(fields, lat_dev, lon_dev)
    )

    local_rows = lat_index * lat_dev + jnp.arange(lat_dev, dtype=jnp.int32)
    up = [(i, i + 1) for i in range(lat_count - 1)]
    down = [(i + 1, i) for i in range(lat_count - 1)]
    east = [(i, (i + 1) % lon_count) for i in range(lon_count)]
    west = [((i + 1) % lon_count, i) for i in range(lon_count)]

    caps = -(-(total_rows // 8) // lat_dev)
    polar_bands = sorted(set(range(caps)) | set(range(lat_count - caps, lat_count)))
    share = fields // lon_count
    lon_index = lax.axis_index("lon")

    def among_polar(block, shift):
        pairs = [
            (band * lon_count + z, band * lon_count + (z + shift) % lon_count)
            for band in polar_bands
            for z in range(lon_count)
        ]
        return lax.ppermute(block, ("lat", "lon"), pairs)

    def own_share(array, shift):
        start = (lon_index + shift) % lon_count * share
        return lax.dynamic_slice_in_dim(array, start, share, axis=0)

    grouped = [own_share(adjoint, 0)]
    for m in range(1, lon_count):
        grouped.append(among_polar(own_share(adjoint, -m), -m))
    lat_ratio = jnp.sin(math.pi * (local_rows.astype(jnp.float32) + 0.5) / total_rows) / math.sin(
        math.pi * (total_rows // 8) / total_rows
    )
    live = lax.dynamic_slice_in_dim(polar_mask, lat_index * lat_dev, lat_dev) > 0
    tables = circle_tables(lon_width)
    blocks = lon_count // 4
    quarters = [
        jnp.concatenate([grouped[blocks * i + j] for j in range(blocks)], axis=2) for i in range(4)
    ]
    quarter = lon_dev * blocks
    sum_even, sum_odd = quarters[0] + quarters[2], quarters[1] + quarters[3]
    pair = jnp.concatenate([quarters[0] - quarters[2], quarters[1] - quarters[3]], axis=2)
    filt = functools.partial(corrected, lat_ratio=lat_ratio, live=live, lon_width=lon_width)
    zero_part = filt(sum_even + sum_odd, *tables[0])
    two_part = filt(sum_even - sum_odd, *tables[1])
    pair_part = filt(pair, *tables[2])
    first, second = pair_part[:, :, :quarter], pair_part[:, :, quarter:]
    even_part, odd_part = zero_part + two_part, zero_part - two_part
    results = [even_part + first, odd_part + second, even_part - first, odd_part - second]
    field = adjoint
    for m in range(lon_count):
        spot = (m % blocks) * lon_dev
        change = results[m // blocks][:, :, spot : spot + lon_dev]
        if m > 0:
            change = among_polar(change, m)
        start = (lon_index - m) % lon_count * share
        field = lax.dynamic_update_slice_in_dim(field, own_share(adjoint, -m) + change, start, axis=0)
    field = field.reshape(tracers, levels, lat_dev, lon_dev)

    from_east = lax.ppermute(field[:, :, :, 0], "lon", west)
    from_west = lax.ppermute(
        jnp.concatenate([field[:, :, :, -1], wind_east[None, :, :, -1]]), "lon", east
    )
    from_north = lax.ppermute(field[:, :, 0, :], "lat", down)
    from_south = lax.ppermute(
        jnp.concatenate([field[:, :, -1, :], wind_north[None, :, -1, :]]), "lat", up
    )
    cols = jnp.concatenate([from_east, from_west]).transpose(1, 2, 0)
    rows_edge = jnp.concatenate([from_north, from_south]).transpose(1, 0, 2)
    keep = (lat_index < lat_count - 1).astype(jnp.int32).reshape(1)
    return advect(keep, field, wind_east, wind_north, cols, rows_edge)


def solution(mesh):
    placed = (
        P(None, None, "lat", "lon"),
        P(None, "lat", "lon"),
        P(None, "lat", "lon"),
        P(),
        P(("lat", "lon"), None),
        P(("lat", "lon")),
        P(("lat", "lon"), None),
        P(("lat", "lon"), None),
    )

    return jax.shard_map(
        shards, mesh=mesh, in_specs=placed, out_specs=P(None, None, "lat", "lon"), check_vma=False
    )
```

```python
import functools
import math

import jax
import jax.numpy as jnp
import numpy as np
from jax import lax
from jax.experimental import pallas as pl
from jax.experimental.pallas import tpu as pltpu
from jax.sharding import PartitionSpec as P

precise_mode = lax.Precision.HIGH
ACCS = 4
UNROLL = 2


def circle_tables(lon_width):
    width = lon_width // 4
    half = width // 2
    inner = 16

    def table(waves, turns, repeats):
        high = np.arange(width // inner)[:, None] * inner
        high = 2.0 * np.pi * ((high * waves[None, :]) % lon_width) / lon_width
        high = np.concatenate([high + 0.5 * np.pi * turn for turn in range(repeats)], 0)
        low = np.arange(inner)[:, None]
        low = 2.0 * np.pi * ((low * waves[None, :]) % lon_width) / lon_width
        low = low - 0.5 * np.pi * turns[None, :]
        parts = [np.cos(high), np.sin(high), np.cos(low), np.sin(low)]
        parts = lax.optimization_barrier([jnp.asarray(part.astype(np.float32)) for part in parts])
        cos_high, sin_high, cos_low, sin_low = parts
        full = cos_high[:, None] * cos_low[None] - sin_high[:, None] * sin_low[None]
        return full.reshape(repeats * width, waves.shape[0])

    zero = np.concatenate([4 * np.arange(half + 1), 4 * np.arange(1, half)])
    zero_turns = np.concatenate([np.zeros(half + 1), np.ones(half - 1)])
    zero_weights = np.where((zero == 0) | (zero == lon_width // 2), 1.0, 2.0)
    two = np.tile(4 * np.arange(half) + 2, 2)
    one = np.tile(4 * np.arange(width) + 1, 2)
    return [
        (table(zero, zero_turns, 1), zero, zero_weights / lon_width),
        (table(two, np.repeat([0, 1], half), 1), two, np.full(width, 2.0 / lon_width)),
        (table(one, np.repeat([0, 1], width), 2), one, np.full(2 * width, 2.0 / lon_width)),
    ]


def corrected(data, basis, waves, weights, lat_ratio, live, lon_width):
    fields, rows, width = data.shape
    sine_k = jnp.asarray(np.sin(np.pi * waves / lon_width).astype(np.float32))
    damping = lat_ratio[:, None] / jnp.maximum(sine_k[None, :], lat_ratio[:, None])
    factor = (damping - 1.0) * jnp.asarray(weights.astype(np.float32))[None, :]
    factor = jnp.where(live[:, None], factor, 0.0)
    spectra = jnp.dot(data.reshape(fields * rows, width), basis, precision=precise_mode)
    spectra = (spectra.reshape(fields, rows, width) * factor[None]).reshape(fields * rows, width)
    result = lax.dot_general(spectra, basis, (((1,), (1,)), ((), ())), precision=precise_mode)
    return result.reshape(fields, rows, width)


def scatter_kernel(cells_ref, values_ref, out_ref, *extra):
    accs = (out_ref,) + extra
    total, width = out_ref.shape
    chunk = 64
    count = values_ref.shape[0]

    def clear(i, carry):
        where = pl.ds(pl.multiple_of(i * chunk, chunk), chunk)
        for acc in accs:
            acc[where, :] = jnp.zeros((chunk, width), jnp.float32)
        return carry

    lax.fori_loop(0, total // chunk, clear, 0)
    step = 2 * ACCS * UNROLL

    def add(i, carry):
        base = i * step
        for turn in range(UNROLL):
            places, news = [], []
            for lane in range(2 * ACCS):
                spot = base + turn * 2 * ACCS + lane
                acc = accs[lane % ACCS]
                place = cells_ref[spot]
                value = values_ref[pl.ds(spot, 1), :]
                if lane >= ACCS:
                    same = jnp.where(place == places[lane - ACCS], 1.0, 0.0)
                    value = value + values_ref[pl.ds(spot - ACCS, 1), :] * same
                places.append(place)
                news.append(acc[pl.ds(place, 1), :] + value)
            for lane in range(2 * ACCS):
                accs[lane % ACCS][pl.ds(places[lane], 1), :] = news[lane]
        return carry

    lax.fori_loop(0, count // step, add, 0)

    def join(i, carry):
        where = pl.ds(pl.multiple_of(i * chunk, chunk), chunk)
        total_here = accs[0][where, :]
        for acc in extra:
            total_here = total_here + acc[where, :]
        out_ref[where, :] = total_here
        return carry

    lax.fori_loop(0, total // chunk, join, 0)


def place_kernel(slots_ref, payload_ref, out_ref):
    chunk = 64

    def clear(i, carry):
        where = pl.ds(pl.multiple_of(i * chunk, chunk), chunk)
        out_ref[where, :] = jnp.zeros((chunk, out_ref.shape[1]), jnp.float32)
        return carry

    lax.fori_loop(0, out_ref.shape[0] // chunk, clear, 0)

    def put(i, carry):
        base = i * 16
        rows = [payload_ref[pl.ds(base + j, 1), :] for j in range(16)]
        slots = [slots_ref[base + j] for j in range(16)]
        for slot, row in zip(slots, rows):
            out_ref[pl.ds(slot, 1), :] = row
        return carry

    lax.fori_loop(0, payload_ref.shape[0] // 16, put, 0)


def place_soundings(slots, payload, total):
    return pl.pallas_call(
        place_kernel,
        out_shape=jax.ShapeDtypeStruct((total, payload.shape[1]), jnp.float32),
        in_specs=[
            pl.BlockSpec(memory_space=pltpu.SMEM),
            pl.BlockSpec(memory_space=pltpu.VMEM),
        ],
        out_specs=pl.BlockSpec(memory_space=pltpu.VMEM),
        compiler_params=pltpu.CompilerParams(vmem_limit_bytes=32 * 1024 * 1024),
    )(slots, payload)


def add_soundings(cells, values, total):
    width = values.shape[1]
    return pl.pallas_call(
        scatter_kernel,
        out_shape=jax.ShapeDtypeStruct((total, width), jnp.float32),
        in_specs=[
            pl.BlockSpec(memory_space=pltpu.SMEM),
            pl.BlockSpec(memory_space=pltpu.VMEM),
        ],
        out_specs=pl.BlockSpec(memory_space=pltpu.VMEM),
        scratch_shapes=[pltpu.VMEM((total, width), jnp.float32)] * (ACCS - 1),
        compiler_params=pltpu.CompilerParams(vmem_limit_bytes=48 * 1024 * 1024),
    )(cells, values)


def stencil_kernel(keep_ref, field_ref, east_ref, north_ref, cols_ref, rows_ref, out_ref, wide, edge):
    tracers, levels, rows, width = field_ref.shape
    padded = wide.shape[1]
    lanes = lax.broadcasted_iota(jnp.int32, (rows, padded), 1)
    subs = lax.broadcasted_iota(jnp.int32, (rows, padded), 0)
    keep = keep_ref[0]

    def widened(slot, block):
        wide[slot * rows : (slot + 1) * rows, 0:width] = block
        return wide[slot * rows : (slot + 1) * rows, :]

    for level in range(levels):
        cols = cols_ref[level]
        edge[0 : 2 * tracers + 1, 0:width] = rows_ref[level]
        wind_east = widened(0, east_ref[level])
        wind_west = jnp.where(
            lanes == 0, cols[:, 2 * tracers : 2 * tracers + 1], pltpu.roll(wind_east, 1, 1)
        )
        wind_north = widened(1, north_ref[level])
        wind_south = jnp.where(
            subs == 0, edge[2 * tracers : 2 * tracers + 1, :], pltpu.roll(wind_north, 1, 0)
        )
        wind_north = jnp.where((subs == rows - 1) & (keep == 0), 0.0, wind_north)
        east_face = jnp.maximum(wind_east, 0.0)
        west_face = jnp.minimum(wind_west, 0.0)
        north_face = jnp.maximum(wind_north, 0.0)
        south_face = jnp.minimum(wind_south, 0.0)
        for tracer in range(tracers):
            other = tracers + tracer
            center = widened(2 + tracer, field_ref[tracer, level])
            east_val = jnp.where(
                lanes == width - 1, cols[:, tracer : tracer + 1], pltpu.roll(center, padded - 1, 1)
            )
            west_val = jnp.where(lanes == 0, cols[:, other : other + 1], pltpu.roll(center, 1, 1))
            upper_val = jnp.where(
                subs == rows - 1, edge[tracer : tracer + 1, :], pltpu.roll(center, rows - 1, 0)
            )
            lower_val = jnp.where(subs == 0, edge[other : other + 1, :], pltpu.roll(center, 1, 0))
            result = center + east_face * (east_val - center) + west_face * (center - west_val)
            result = result + north_face * (upper_val - center) + south_face * (center - lower_val)
            out_ref[tracer, level] = result[:, 0:width]


def advect(keep, field, wind_east, wind_north, cols, rows_edge):
    tracers, levels, rows, width = field.shape
    step = 4 if levels % 4 == 0 else 1
    padded = -(-(width + 1) // 128) * 128
    edges = 2 * tracers + 1

    def four(depth, span):
        return pl.BlockSpec((tracers, step, depth, span), lambda i: (0, i, 0, 0))

    def three(depth, span):
        return pl.BlockSpec((step, depth, span), lambda i: (i, 0, 0))

    return pl.pallas_call(
        stencil_kernel,
        grid=(levels // step,),
        out_shape=jax.ShapeDtypeStruct(field.shape, jnp.float32),
        in_specs=[
            pl.BlockSpec(memory_space=pltpu.SMEM),
            four(rows, width), three(rows, width), three(rows, width),
            three(rows, edges), three(edges, width),
        ],
        out_specs=four(rows, width),
        scratch_shapes=[
            pltpu.VMEM(((2 + tracers) * rows, padded), jnp.float32),
            pltpu.VMEM((8, padded), jnp.float32),
        ],
        compiler_params=pltpu.CompilerParams(vmem_limit_bytes=32 * 1024 * 1024),
    )(keep, field, wind_east, wind_north, cols, rows_edge)


def owner_positions(owner_dev, devices):
    count = owner_dev.shape[0]
    span = 128
    one_hot = (owner_dev[:, None] == lax.broadcasted_iota(jnp.int32, (1, devices), 1)).astype(
        jnp.bfloat16
    ).reshape(count // span, span, devices)
    lower = jnp.asarray(np.tril(np.ones((span, span))), jnp.bfloat16)
    inner = jnp.einsum("ij,bjd->bid", lower, one_hot, preferred_element_type=jnp.float32)
    sums = inner[:, -1, :]
    blocks = count // span
    before = jnp.asarray(np.tril(np.ones((blocks, blocks)), -1), jnp.float32)
    offset = jnp.dot(before, sums, precision=lax.Precision.HIGHEST)
    ranks = (inner + offset[:, None, :]) * one_hot.astype(jnp.float32)
    return jnp.sum(ranks, axis=2).reshape(count).astype(jnp.int32) - 1


def shards(
    adjoint_in, wind_east, wind_north, polar_mask, obs_owner, obs_cell, obs_kernel, obs_resid
):
    tracers, levels, lat_dev, lon_dev = adjoint_in.shape
    fields = tracers * levels
    lat_count = lax.axis_size("lat")
    lon_count = lax.axis_size("lon")
    lat_index = lax.axis_index("lat")
    lon_width = lon_dev * lon_count
    total_rows = lat_dev * lat_count
    devices = lat_count * lon_count
    obs_count = obs_owner.shape[0]
    capacity = 2 * obs_count // devices

    owner_dev = obs_owner[:, 0]
    slot_index = owner_dev * capacity + owner_positions(owner_dev, devices)
    payload = jnp.concatenate(
        [
            obs_kernel,
            obs_resid,
            obs_cell.astype(jnp.float32)[:, None],
            jnp.zeros((obs_count, 32 - levels - tracers - 1), jnp.float32),
        ],
        axis=1,
    )
    send = place_soundings(slot_index, payload, devices * capacity)
    got = lax.all_to_all(
        send.reshape(devices, capacity, 32), ("lat", "lon"), split_axis=0, concat_axis=0, tiled=True
    ).reshape(devices * capacity, 32)
    tables = circle_tables(lon_width)
    got, bases = lax.optimization_barrier((got, [table[0] for table in tables]))
    tables = [(basis,) + table[1:] for basis, table in zip(bases, tables)]
    got_cells = got[:, levels + tracers].astype(jnp.int32)
    got_values = (
        got[:, levels : levels + tracers, None] * got[:, None, :levels]
    ).reshape(devices * capacity, fields)
    forcing = add_soundings(got_cells, got_values, lat_dev * lon_dev)
    adjoint = (
        adjoint_in.reshape(fields, lat_dev, lon_dev)
        + forcing.T.reshape(fields, lat_dev, lon_dev)
    )

    local_rows = lat_index * lat_dev + jnp.arange(lat_dev, dtype=jnp.int32)
    up = [(i, i + 1) for i in range(lat_count - 1)]
    down = [(i + 1, i) for i in range(lat_count - 1)]
    east = [(i, (i + 1) % lon_count) for i in range(lon_count)]
    west = [((i + 1) % lon_count, i) for i in range(lon_count)]

    caps = -(-(total_rows // 8) // lat_dev)
    polar_bands = sorted(set(range(caps)) | set(range(lat_count - caps, lat_count)))
    share = fields // lon_count
    lon_index = lax.axis_index("lon")

    def among_polar(block, shift):
        pairs = [
            (band * lon_count + z, band * lon_count + (z + shift) % lon_count)
            for band in polar_bands
            for z in range(lon_count)
        ]
        return lax.ppermute(block, ("lat", "lon"), pairs)

    def own_share(array, shift):
        start = (lon_index + shift) % lon_count * share
        return lax.dynamic_slice_in_dim(array, start, share, axis=0)

    shares = lax.optimization_barrier([own_share(adjoint, -m) for m in range(lon_count)])
    grouped = [among_polar(block, -m) if m else block for m, block in enumerate(shares)]
    lat_ratio = jnp.sin(math.pi * (local_rows.astype(jnp.float32) + 0.5) / total_rows) / math.sin(
        math.pi * (total_rows // 8) / total_rows
    )
    live = lax.dynamic_slice_in_dim(polar_mask, lat_index * lat_dev, lat_dev) > 0
    blocks = lon_count // 4
    quarters = [
        jnp.concatenate([grouped[blocks * i + j] for j in range(blocks)], axis=2) for i in range(4)
    ]
    quarter = lon_dev * blocks
    sum_even, sum_odd = quarters[0] + quarters[2], quarters[1] + quarters[3]
    pair = jnp.concatenate([quarters[0] - quarters[2], quarters[1] - quarters[3]], axis=2)
    filt = functools.partial(corrected, lat_ratio=lat_ratio, live=live, lon_width=lon_width)
    zero_part = filt(sum_even + sum_odd, *tables[0])
    two_part = filt(sum_even - sum_odd, *tables[1])
    pair_part = filt(pair, *tables[2])
    first, second = pair_part[:, :, :quarter], pair_part[:, :, quarter:]
    even_part, odd_part = zero_part + two_part, zero_part - two_part
    results = [even_part + first, odd_part + second, even_part - first, odd_part - second]
    field = adjoint
    for m in range(lon_count):
        spot = (m % blocks) * lon_dev
        change = results[m // blocks][:, :, spot : spot + lon_dev]
        if m > 0:
            change = among_polar(change, m)
        start = (lon_index - m) % lon_count * share
        field = lax.dynamic_update_slice_in_dim(field, own_share(adjoint, -m) + change, start, axis=0)
    field = field.reshape(tracers, levels, lat_dev, lon_dev)

    from_east = lax.ppermute(field[:, :, :, 0], "lon", west)
    from_west = lax.ppermute(
        jnp.concatenate([field[:, :, :, -1], wind_east[None, :, :, -1]]), "lon", east
    )
    from_north = lax.ppermute(field[:, :, 0, :], "lat", down)
    from_south = lax.ppermute(
        jnp.concatenate([field[:, :, -1, :], wind_north[None, :, -1, :]]), "lat", up
    )
    cols = jnp.concatenate([from_east, from_west]).transpose(1, 2, 0)
    rows_edge = jnp.concatenate([from_north, from_south]).transpose(1, 0, 2)
    keep = (lat_index < lat_count - 1).astype(jnp.int32).reshape(1)
    return advect(keep, field, wind_east, wind_north, cols, rows_edge)


def solution(mesh):
    placed = (
        P(None, None, "lat", "lon"),
        P(None, "lat", "lon"),
        P(None, "lat", "lon"),
        P(),
        P(("lat", "lon"), None),
        P(("lat", "lon")),
        P(("lat", "lon"), None),
        P(("lat", "lon"), None),
    )

    return jax.shard_map(
        shards, mesh=mesh, in_specs=placed, out_specs=P(None, None, "lat", "lon"), check_vma=False
    )
```

```python
import functools
import math

import jax
import jax.numpy as jnp
import numpy as np
from jax import lax
from jax.experimental import pallas as pl
from jax.experimental.pallas import tpu as pltpu
from jax.sharding import PartitionSpec as P

precise_mode = lax.Precision.HIGH
ACCS = 4
UNROLL = 2


def circle_tables(lon_width):
    width = lon_width // 4
    half = width // 2
    inner = 16

    def table(waves, turns, repeats):
        high = np.arange(width // inner)[:, None] * inner
        high = 2.0 * np.pi * ((high * waves[None, :]) % lon_width) / lon_width
        high = np.concatenate([high + 0.5 * np.pi * turn for turn in range(repeats)], 0)
        low = np.arange(inner)[:, None]
        low = 2.0 * np.pi * ((low * waves[None, :]) % lon_width) / lon_width
        low = low - 0.5 * np.pi * turns[None, :]
        parts = [np.cos(high), np.sin(high), np.cos(low), np.sin(low)]
        parts = lax.optimization_barrier([jnp.asarray(part.astype(np.float32)) for part in parts])
        cos_high, sin_high, cos_low, sin_low = parts
        full = cos_high[:, None] * cos_low[None] - sin_high[:, None] * sin_low[None]
        return full.reshape(repeats * width, waves.shape[0])

    zero = np.concatenate([4 * np.arange(half + 1), 4 * np.arange(1, half)])
    zero_turns = np.concatenate([np.zeros(half + 1), np.ones(half - 1)])
    zero_weights = np.where((zero == 0) | (zero == lon_width // 2), 1.0, 2.0)
    two = np.tile(4 * np.arange(half) + 2, 2)
    one = np.tile(4 * np.arange(width) + 1, 2)
    return [
        (table(zero, zero_turns, 1), zero, zero_weights / lon_width),
        (table(two, np.repeat([0, 1], half), 1), two, np.full(width, 2.0 / lon_width)),
        (table(one, np.repeat([0, 1], width), 2), one, np.full(2 * width, 2.0 / lon_width)),
    ]


def corrected(data, basis, waves, weights, lat_ratio, live, lon_width):
    fields, rows, width = data.shape
    sine_k = jnp.asarray(np.sin(np.pi * waves / lon_width).astype(np.float32))
    damping = lat_ratio[:, None] / jnp.maximum(sine_k[None, :], lat_ratio[:, None])
    factor = (damping - 1.0) * jnp.asarray(weights.astype(np.float32))[None, :]
    factor = jnp.where(live[:, None], factor, 0.0)
    spectra = jnp.dot(data.reshape(fields * rows, width), basis, precision=precise_mode)
    spectra = (spectra.reshape(fields, rows, width) * factor[None]).reshape(fields * rows, width)
    result = lax.dot_general(spectra, basis, (((1,), (1,)), ((), ())), precision=precise_mode)
    return result.reshape(fields, rows, width)


def scatter_kernel(cells_ref, values_ref, out_ref, *extra):
    accs = (out_ref,) + extra
    total, width = out_ref.shape
    chunk = 64
    count = values_ref.shape[0]

    def clear(i, carry):
        where = pl.ds(pl.multiple_of(i * chunk, chunk), chunk)
        for acc in accs:
            acc[where, :] = jnp.zeros((chunk, width), jnp.float32)
        return carry

    lax.fori_loop(0, total // chunk, clear, 0)
    step = 8 * UNROLL

    def add(i, carry):
        for turn in range(UNROLL):
            base = pl.multiple_of(i * step + turn * 8, 8)
            block = values_ref[pl.ds(base, 8), :]
            for first in range(0, 8, ACCS):
                places = [cells_ref[base + first + lane] for lane in range(ACCS)]
                news = [
                    accs[lane][pl.ds(places[lane], 1), :] + block[first + lane : first + lane + 1, :]
                    for lane in range(ACCS)
                ]
                for lane in range(ACCS):
                    accs[lane][pl.ds(places[lane], 1), :] = news[lane]
        return carry

    lax.fori_loop(0, count // step, add, 0)

    def join(i, carry):
        where = pl.ds(pl.multiple_of(i * chunk, chunk), chunk)
        total_here = accs[0][where, :]
        for acc in extra:
            total_here = total_here + acc[where, :]
        out_ref[where, :] = total_here
        return carry

    lax.fori_loop(0, total // chunk, join, 0)


def place_kernel(slots_ref, payload_ref, out_ref):
    chunk = 64

    def clear(i, carry):
        where = pl.ds(pl.multiple_of(i * chunk, chunk), chunk)
        out_ref[where, :] = jnp.zeros((chunk, out_ref.shape[1]), jnp.float32)
        return carry

    lax.fori_loop(0, out_ref.shape[0] // chunk, clear, 0)

    def put(i, carry):
        base = pl.multiple_of(i * 16, 16)
        block = payload_ref[pl.ds(base, 16), :]
        slots = [slots_ref[base + j] for j in range(16)]
        for j, slot in enumerate(slots):
            out_ref[pl.ds(slot, 1), :] = block[j : j + 1, :]
        return carry

    lax.fori_loop(0, payload_ref.shape[0] // 16, put, 0)


def place_soundings(slots, payload, total):
    return pl.pallas_call(
        place_kernel,
        out_shape=jax.ShapeDtypeStruct((total, payload.shape[1]), jnp.float32),
        in_specs=[
            pl.BlockSpec(memory_space=pltpu.SMEM),
            pl.BlockSpec(memory_space=pltpu.VMEM),
        ],
        out_specs=pl.BlockSpec(memory_space=pltpu.VMEM),
        compiler_params=pltpu.CompilerParams(vmem_limit_bytes=32 * 1024 * 1024),
    )(slots, payload)


def add_soundings(cells, values, total):
    width = values.shape[1]
    return pl.pallas_call(
        scatter_kernel,
        out_shape=jax.ShapeDtypeStruct((total, width), jnp.float32),
        in_specs=[
            pl.BlockSpec(memory_space=pltpu.SMEM),
            pl.BlockSpec(memory_space=pltpu.VMEM),
        ],
        out_specs=pl.BlockSpec(memory_space=pltpu.VMEM),
        scratch_shapes=[pltpu.VMEM((total, width), jnp.float32)] * (ACCS - 1),
        compiler_params=pltpu.CompilerParams(vmem_limit_bytes=48 * 1024 * 1024),
    )(cells, values)


def stencil_kernel(keep_ref, field_ref, east_ref, north_ref, cols_ref, rows_ref, out_ref, wide, edge):
    tracers, levels, rows, width = field_ref.shape
    padded = wide.shape[1]
    lanes = lax.broadcasted_iota(jnp.int32, (rows, padded), 1)
    subs = lax.broadcasted_iota(jnp.int32, (rows, padded), 0)
    keep = keep_ref[0]

    def widened(slot, block):
        wide[slot * rows : (slot + 1) * rows, 0:width] = block
        return wide[slot * rows : (slot + 1) * rows, :]

    for level in range(levels):
        cols = cols_ref[level]
        edge[0 : 2 * tracers + 1, 0:width] = rows_ref[level]
        wind_east = widened(0, east_ref[level])
        wind_west = jnp.where(
            lanes == 0, cols[:, 2 * tracers : 2 * tracers + 1], pltpu.roll(wind_east, 1, 1)
        )
        wind_north = widened(1, north_ref[level])
        wind_south = jnp.where(
            subs == 0, edge[2 * tracers : 2 * tracers + 1, :], pltpu.roll(wind_north, 1, 0)
        )
        wind_north = jnp.where((subs == rows - 1) & (keep == 0), 0.0, wind_north)
        east_face = jnp.maximum(wind_east, 0.0)
        west_face = jnp.minimum(wind_west, 0.0)
        north_face = jnp.maximum(wind_north, 0.0)
        south_face = jnp.minimum(wind_south, 0.0)
        for tracer in range(tracers):
            other = tracers + tracer
            center = widened(2 + tracer, field_ref[tracer, level])
            east_val = jnp.where(
                lanes == width - 1, cols[:, tracer : tracer + 1], pltpu.roll(center, padded - 1, 1)
            )
            west_val = jnp.where(lanes == 0, cols[:, other : other + 1], pltpu.roll(center, 1, 1))
            upper_val = jnp.where(
                subs == rows - 1, edge[tracer : tracer + 1, :], pltpu.roll(center, rows - 1, 0)
            )
            lower_val = jnp.where(subs == 0, edge[other : other + 1, :], pltpu.roll(center, 1, 0))
            result = center + east_face * (east_val - center) + west_face * (center - west_val)
            result = result + north_face * (upper_val - center) + south_face * (center - lower_val)
            out_ref[tracer, level] = result[:, 0:width]


def advect(keep, field, wind_east, wind_north, cols, rows_edge):
    tracers, levels, rows, width = field.shape
    step = 4 if levels % 4 == 0 else 1
    padded = -(-(width + 1) // 128) * 128
    edges = 2 * tracers + 1

    def four(depth, span):
        return pl.BlockSpec((tracers, step, depth, span), lambda i: (0, i, 0, 0))

    def three(depth, span):
        return pl.BlockSpec((step, depth, span), lambda i: (i, 0, 0))

    return pl.pallas_call(
        stencil_kernel,
        grid=(levels // step,),
        out_shape=jax.ShapeDtypeStruct(field.shape, jnp.float32),
        in_specs=[
            pl.BlockSpec(memory_space=pltpu.SMEM),
            four(rows, width), three(rows, width), three(rows, width),
            three(rows, edges), three(edges, width),
        ],
        out_specs=four(rows, width),
        scratch_shapes=[
            pltpu.VMEM(((2 + tracers) * rows, padded), jnp.float32),
            pltpu.VMEM((8, padded), jnp.float32),
        ],
        compiler_params=pltpu.CompilerParams(vmem_limit_bytes=32 * 1024 * 1024),
    )(keep, field, wind_east, wind_north, cols, rows_edge)


def owner_positions(owner_dev, devices):
    count = owner_dev.shape[0]
    span = 128
    one_hot = (owner_dev[:, None] == lax.broadcasted_iota(jnp.int32, (1, devices), 1)).astype(
        jnp.bfloat16
    ).reshape(count // span, span, devices)
    lower = jnp.asarray(np.tril(np.ones((span, span))), jnp.bfloat16)
    inner = jnp.einsum("ij,bjd->bid", lower, one_hot, preferred_element_type=jnp.float32)
    sums = inner[:, -1, :]
    blocks = count // span
    before = jnp.asarray(np.tril(np.ones((blocks, blocks)), -1), jnp.float32)
    offset = jnp.dot(before, sums, precision=lax.Precision.HIGHEST)
    ranks = (inner + offset[:, None, :]) * one_hot.astype(jnp.float32)
    return jnp.sum(ranks, axis=2).reshape(count).astype(jnp.int32) - 1


def shards(
    adjoint_in, wind_east, wind_north, polar_mask, obs_owner, obs_cell, obs_kernel, obs_resid
):
    tracers, levels, lat_dev, lon_dev = adjoint_in.shape
    fields = tracers * levels
    lat_count = lax.axis_size("lat")
    lon_count = lax.axis_size("lon")
    lat_index = lax.axis_index("lat")
    lon_width = lon_dev * lon_count
    total_rows = lat_dev * lat_count
    devices = lat_count * lon_count
    obs_count = obs_owner.shape[0]
    capacity = 2 * obs_count // devices

    owner_dev = obs_owner[:, 0]
    slot_index = owner_dev * capacity + owner_positions(owner_dev, devices)
    payload = jnp.concatenate(
        [
            obs_kernel,
            obs_resid,
            obs_cell.astype(jnp.float32)[:, None],
            jnp.zeros((obs_count, 32 - levels - tracers - 1), jnp.float32),
        ],
        axis=1,
    )
    send = place_soundings(slot_index, payload, devices * capacity)
    got = lax.all_to_all(
        send.reshape(devices, capacity, 32), ("lat", "lon"), split_axis=0, concat_axis=0, tiled=True
    ).reshape(devices * capacity, 32)
    tables = circle_tables(lon_width)
    got, bases = lax.optimization_barrier((got, [table[0] for table in tables]))
    tables = [(basis,) + table[1:] for basis, table in zip(bases, tables)]
    got_cells = got[:, levels + tracers].astype(jnp.int32)
    got_values = (
        got[:, levels : levels + tracers, None] * got[:, None, :levels]
    ).reshape(devices * capacity, fields)
    forcing = add_soundings(got_cells, got_values, lat_dev * lon_dev)
    adjoint = (
        adjoint_in.reshape(fields, lat_dev, lon_dev)
        + forcing.T.reshape(fields, lat_dev, lon_dev)
    )

    local_rows = lat_index * lat_dev + jnp.arange(lat_dev, dtype=jnp.int32)
    up = [(i, i + 1) for i in range(lat_count - 1)]
    down = [(i + 1, i) for i in range(lat_count - 1)]
    east = [(i, (i + 1) % lon_count) for i in range(lon_count)]
    west = [((i + 1) % lon_count, i) for i in range(lon_count)]

    caps = -(-(total_rows // 8) // lat_dev)
    polar_bands = sorted(set(range(caps)) | set(range(lat_count - caps, lat_count)))
    share = fields // lon_count
    lon_index = lax.axis_index("lon")

    def among_polar(block, shift):
        pairs = [
            (band * lon_count + z, band * lon_count + (z + shift) % lon_count)
            for band in polar_bands
            for z in range(lon_count)
        ]
        return lax.ppermute(block, ("lat", "lon"), pairs)

    def own_share(array, shift):
        start = (lon_index + shift) % lon_count * share
        return lax.dynamic_slice_in_dim(array, start, share, axis=0)

    shares = lax.optimization_barrier([own_share(adjoint, -m) for m in range(lon_count)])
    grouped = [among_polar(block, -m) if m else block for m, block in enumerate(shares)]
    lat_ratio = jnp.sin(math.pi * (local_rows.astype(jnp.float32) + 0.5) / total_rows) / math.sin(
        math.pi * (total_rows // 8) / total_rows
    )
    live = lax.dynamic_slice_in_dim(polar_mask, lat_index * lat_dev, lat_dev) > 0
    blocks = lon_count // 4
    quarters = [
        jnp.concatenate([grouped[blocks * i + j] for j in range(blocks)], axis=2) for i in range(4)
    ]
    quarter = lon_dev * blocks
    sum_even, sum_odd = quarters[0] + quarters[2], quarters[1] + quarters[3]
    pair = jnp.concatenate([quarters[0] - quarters[2], quarters[1] - quarters[3]], axis=2)
    filt = functools.partial(corrected, lat_ratio=lat_ratio, live=live, lon_width=lon_width)
    zero_part = filt(sum_even + sum_odd, *tables[0])
    two_part = filt(sum_even - sum_odd, *tables[1])
    pair_part = filt(pair, *tables[2])
    first, second = pair_part[:, :, :quarter], pair_part[:, :, quarter:]
    even_part, odd_part = zero_part + two_part, zero_part - two_part
    results = [even_part + first, odd_part + second, even_part - first, odd_part - second]
    field = adjoint
    for m in range(lon_count):
        spot = (m % blocks) * lon_dev
        change = results[m // blocks][:, :, spot : spot + lon_dev]
        if m > 0:
            change = among_polar(change, m)
        start = (lon_index - m) % lon_count * share
        field = lax.dynamic_update_slice_in_dim(field, own_share(adjoint, -m) + change, start, axis=0)
    field = field.reshape(tracers, levels, lat_dev, lon_dev)

    from_east = lax.ppermute(field[:, :, :, 0], "lon", west)
    from_west = lax.ppermute(
        jnp.concatenate([field[:, :, :, -1], wind_east[None, :, :, -1]]), "lon", east
    )
    from_north = lax.ppermute(field[:, :, 0, :], "lat", down)
    from_south = lax.ppermute(
        jnp.concatenate([field[:, :, -1, :], wind_north[None, :, -1, :]]), "lat", up
    )
    cols = jnp.concatenate([from_east, from_west]).transpose(1, 2, 0)
    rows_edge = jnp.concatenate([from_north, from_south]).transpose(1, 0, 2)
    keep = (lat_index < lat_count - 1).astype(jnp.int32).reshape(1)
    return advect(keep, field, wind_east, wind_north, cols, rows_edge)


def solution(mesh):
    placed = (
        P(None, None, "lat", "lon"),
        P(None, "lat", "lon"),
        P(None, "lat", "lon"),
        P(),
        P(("lat", "lon"), None),
        P(("lat", "lon")),
        P(("lat", "lon"), None),
        P(("lat", "lon"), None),
    )

    return jax.shard_map(
        shards, mesh=mesh, in_specs=placed, out_specs=P(None, None, "lat", "lon"), check_vma=False
    )
```
